32 devices in a mesh: row: 4 (over x, core), col: 8 (over z, y).
Axes of the slice: x: 2, y: 2, z: 4, core: 2. Of those that a mesh axis runs over, the one named last changes fastest.
Arguments:
- integrals: bfloat16 [384, 64, 4096], P(('row', 'col')), may hold values from -6 to 6
- block_list: int32 [384, 3], P(('row', 'col')), may hold values from 0 to 31, as said below
- p_slot: int32 [16], replicated, may hold values from 0 to 15, as said below
- metric: bfloat16 [16, 64, 64], P('col'), may hold values from -0.75 to 0.75
- density_panel: bfloat16 [2048, 128], P(('row', 'col')), may hold values from -0.75 to 0.75
- pattern: int32 [2048], P(('row', 'col')), may hold values 0 or 1
Outputs:
- exchange_blocks: float32 [2048, 512], P(('row', 'col'))
The draws below stay inside these ranges and needn't reach their ends.
Inputs may be any that keep to these rules, and one draw needn't show every extreme that they name: `block_list`: rows name (mu block, nu block, auxiliary block). The 12 rows of the device at position row * 8 + col have mu blocks in row * 8 to row * 8 + 7. With owner p_slot[p] // 2, no device lists more than 2 blocks for one owner, and in every row group some owner gets exactly 2 from every device of the group. A permutation; auxiliary block p is contracted by col index p_slot[p] // 2, local slot p_slot[p] % 2.
All inputs are finite; a program needn't handle non-finite values. No bound on the sum of `pattern` on one device may be relied on, other than what follows from the above.
Results may differ from the reference program's by a relative error of at most 0.00059.
Values may be sent and summed in bfloat16 or wider, within the bound.
A program may use at most 192 MiB of HBM per device.

```python
import jax
import jax.numpy as jnp
from jax import lax

BS = 64
MB = 8
PB = 2
OCC = 128
E_DEV = 12
NBLK = 32
NPB = 16
ORBS = 2048
BLOCKS = 384
N_ROW = 4
N_COL = 8


def slot_order(key):
    return jax.random.permutation(jax.random.fold_in(key, 11), NPB).astype(jnp.int32)


def draw_p_slot(key, part):
    return slot_order(key)


def draw_block_list(key, part):
    ordering = slot_order(key)
    inverse = jnp.argsort(ordering, stable=True).astype(jnp.int32)
    devices = N_ROW * N_COL
    draw_key = jax.random.fold_in(key, 23)
    row_of_device = jnp.arange(devices, dtype=jnp.int32) // N_COL
    favored = jax.random.randint(jax.random.fold_in(draw_key, 1), (N_ROW,), 0, N_COL).astype(jnp.int32)
    device_keys = jax.random.split(jax.random.fold_in(draw_key, 2), devices)
    orders = jax.vmap(lambda k: jax.random.permutation(k, N_COL))(device_keys).astype(jnp.int32)
    starred = favored[row_of_device]
    star_place = jnp.argmax(orders == starred[:, None], axis=1)
    leading = orders[:, 0]
    positions = jnp.arange(N_COL, dtype=jnp.int32)[None, :]
    orders = jnp.where(positions == star_place[:, None], leading[:, None], orders)
    orders = jnp.where(positions == 0, starred[:, None], orders)
    pick_index = jnp.arange(E_DEV, dtype=jnp.int32) % N_COL
    owners = orders[:, pick_index]
    local_slot = jax.random.randint(jax.random.fold_in(draw_key, 3), (devices, E_DEV), 0, PB).astype(jnp.int32)
    fitting = inverse[owners * PB + local_slot]
    first_blocks = row_of_device[:, None] * MB + jax.random.randint(jax.random.fold_in(draw_key, 4), (devices, E_DEV), 0, MB).astype(jnp.int32)
    second_blocks = jax.random.randint(jax.random.fold_in(draw_key, 5), (devices, E_DEV), 0, NBLK).astype(jnp.int32)
    return jnp.stack([first_blocks, second_blocks, fitting], axis=-1).reshape(devices * E_DEV, 3).astype(jnp.int32)


def with_ends(array, rng, low, largest):
    longest = array.shape.index(max(array.shape))
    spots = []
    for shift in (0, 1):
        where = [jax.random.randint(jax.random.fold_in(rng, axis), (), 0, length) for axis, length in enumerate(array.shape)]
        where[longest] = (where[longest] + shift) % array.shape[longest]
        spots.append(tuple(where))
    return array.at[spots[0]].set(low).at[spots[1]].set(largest)


def levels(key, extent, shards, low, high):
    loudness, own = 1.0, jax.random.fold_in(key, 6)
    for axis_at, shards_of in shards:
        steps = jnp.exp(jax.random.uniform(jax.random.fold_in(own, axis_at), (shards_of,), jnp.float32, low / len(shards), high / len(shards)))
        loudness = loudness * jnp.repeat(steps, extent[axis_at] // shards_of).reshape([-1 if axis == axis_at else 1 for axis in range(len(extent))])
    return loudness


def scatter_about(own_key, extent, spread, limit, pieces=(), kind=jnp.bfloat16):
    array = spread * jax.random.normal(own_key, extent, jnp.float32)
    if pieces:
        array = array * levels(own_key, extent, pieces, -0.22, 0.18)
    return jnp.clip(array, -limit, limit).astype(kind)


def setup_inputs(seed: int = 0) -> dict:
    splits = jax.random.split(jax.random.key(seed), 7)
    return {
        "integrals": scatter_about(splits[0], (BLOCKS, BS, BS * BS), 1.0, 6.0, ((0, 32),)),
        "block_list": draw_block_list(jax.random.fold_in(splits[6], 71), 0),
        "p_slot": draw_p_slot(jax.random.fold_in(splits[6], 71), 0),
        "metric": scatter_about(splits[3], (NPB, BS, BS), BS ** -0.5, 0.75, ((0, 8),)),
        "density_panel": scatter_about(splits[4], (ORBS, OCC), BS ** -0.5, 0.75, ((0, 32),)),
        "pattern": with_ends((jax.random.randint(splits[5], (ORBS,), 0, 4) < 3).astype(jnp.int32), jax.random.fold_in(splits[5], 1), 0, 1),
    }


def reference(integrals, block_list, p_slot, metric, density_panel, pattern):
    masked = jnp.where(pattern[:, None] > 0, density_panel, jnp.zeros_like(density_panel))
    panels = masked.reshape(NBLK, BS, OCC)
    slots_all = p_slot[block_list[:, 2]]
    per_group = N_COL * E_DEV
    factor = 1.0 / (NPB * BS * OCC)

    def one_group(group_index):
        first_row = group_index * per_group
        blocks_here = lax.dynamic_slice_in_dim(integrals, first_row, per_group, 0)
        lists_here = lax.dynamic_slice_in_dim(block_list, first_row, per_group, 0)
        slots_here = lax.dynamic_slice_in_dim(slots_all, first_row, per_group, 0)

        def accumulate(running, inputs_now):
            one_block, entry_ids, target = inputs_now
            offset = ((entry_ids[0] - group_index * MB) * BS).astype(jnp.int32)
            applied = jnp.einsum("qp,qx->px", metric[target].astype(jnp.float32), one_block.astype(jnp.float32)).astype(jnp.bfloat16)
            applied = lax.optimization_barrier(applied).astype(jnp.float32).reshape(BS, BS, BS)
            contrib = jnp.einsum("pmn,no->pmo", applied, panels[entry_ids[1]].astype(jnp.float32))
            anchor = jnp.zeros((), jnp.int32)
            corner = (target.astype(jnp.int32), anchor, offset, anchor)
            current = lax.dynamic_slice(running, corner, (1, BS, BS, OCC))
            return lax.dynamic_update_slice(running, current + contrib[None], corner), None

        empty_sum = jnp.zeros((NPB, BS, MB * BS, OCC), jnp.float32)
        filled, _ = lax.scan(accumulate, empty_sum, (blocks_here, lists_here, slots_here))
        rounded = lax.optimization_barrier(filled.astype(jnp.bfloat16)).astype(jnp.float32)
        return jnp.einsum("jpxo,jpzo->xz", rounded, rounded) * factor

    row_tiles = lax.map(one_group, jnp.arange(N_ROW, dtype=jnp.int32))
    return row_tiles.reshape(N_ROW * MB * BS, MB * BS)
```

```python
import functools

import jax
import jax.numpy as jnp
from jax import lax
from jax.experimental import pallas as pl
from jax.experimental.pallas import tpu as pltpu
from jax.sharding import PartitionSpec as P

MB = 8
LANES = 128
DEPTH = 2
MESH = pl.DeviceIdType.MESH
ANY = pl.BlockSpec(memory_space=pl.ANY)
VMEM = pl.BlockSpec(memory_space=pltpu.VMEM)
SMEM = pl.BlockSpec(memory_space=pltpu.SMEM)


def spread_kernel(axis, count, *refs):
    sources, targets = refs[:count], refs[count : 2 * count]
    sends, recvs, local = refs[2 * count :]
    me = lax.axis_index(axis)
    others = range(1, lax.axis_size(axis))

    def device(b):
        return {axis: lax.bitwise_xor(me, b)}

    barrier = pltpu.get_barrier_semaphore()
    for b in others:
        pl.semaphore_signal(barrier, inc=1, device_id=device(b), device_id_type=MESH)
    own = [
        pltpu.make_async_copy(source, target.at[me], local.at[k])
        for k, (source, target) in enumerate(zip(sources, targets))
    ]
    for copy in own:
        copy.start()
    pl.semaphore_wait(barrier, len(others))
    copies = []
    for k, (source, target) in enumerate(zip(sources, targets)):
        for b in others:
            copies.append(pltpu.make_async_remote_copy(
                source, target.at[me], sends.at[k, b], recvs.at[k, b],
                device_id=device(b), device_id_type=MESH))
            copies[-1].start()
    for copy in own + copies:
        copy.wait()


def spread(axis, size, number, arrays):
    count = len(arrays)
    return pl.pallas_call(
        functools.partial(spread_kernel, axis, count),
        out_shape=tuple(jax.ShapeDtypeStruct((size,) + a.shape, a.dtype) for a in arrays),
        in_specs=[VMEM] * count,
        out_specs=(VMEM,) * count,
        scratch_shapes=[
            pltpu.SemaphoreType.DMA((count, size)),
            pltpu.SemaphoreType.DMA((count, size)),
            pltpu.SemaphoreType.DMA((count,)),
        ],
        compiler_params=pltpu.CompilerParams(collective_id=number, has_side_effects=True),
        name="spread_" + axis,
    )(*arrays)


def apply_kernel(cols, depth, slot_ref, pick_ref, metric_ref, block_ref, *refs):
    outs, chosen, turned = refs[:cols], refs[cols], refs[cols + 1]
    lines = block_ref.shape[2] // LANES
    here = block_ref.shape[0]

    @pl.when(pl.program_id(0) == 0)
    def _():
        for e in range(chosen.shape[0]):
            chosen[e] = lax.dot_general(
                pick_ref[...], metric_ref[slot_ref[e]], (((1,), (1,)), ((), ())),
                preferred_element_type=jnp.float32).astype(jnp.bfloat16)

    for k in range(here):
        made = jnp.dot(
            chosen[pl.program_id(0) * here + k], block_ref[k], preferred_element_type=jnp.float32)
        total = made.shape[0]
        for start in range(0, total, 8):
            size = min(8, total - start)
            for line in range(lines):
                turned[k, pl.ds(start * lines + line, size, stride=lines), :] = made[
                    start : start + size, line * LANES : (line + 1) * LANES]
        for d in range(cols):
            for i in range(depth):
                row = (d * depth + i) * lines
                outs[d][i, k] = turned[k, row : row + lines, :].astype(jnp.bfloat16)


def apply_metric(cols, slot_ids, pick, metrics, integrals):
    listed, block_size, flat = integrals.shape
    lines = flat // LANES
    depth = pick.shape[0] // cols
    here = 3 if listed % 3 == 0 else 1
    shape = jax.ShapeDtypeStruct((depth, listed, lines, LANES), jnp.bfloat16)
    return pl.pallas_call(
        functools.partial(apply_kernel, cols, depth),
        grid=(listed // here,),
        out_shape=(shape,) * cols,
        in_specs=[SMEM, VMEM, VMEM, pl.BlockSpec((here, block_size, flat), lambda e: (e, 0, 0))],
        out_specs=(pl.BlockSpec((depth, here, lines, LANES), lambda e: (0, e, 0, 0)),) * cols,
        scratch_shapes=[
            pltpu.VMEM((listed, cols * depth, block_size), jnp.bfloat16),
            pltpu.VMEM((here, cols * depth * lines, LANES), jnp.float32),
        ],
        cost_estimate=pl.CostEstimate(flops=10**9, bytes_accessed=8 * 2**20, transcendentals=0),
        name="apply_metric",
    )(slot_ids, pick, metrics, integrals)


def build_kernel(cols, sizes, first, scale, corner_ref, second_ref, panel_ref, tile_ref, *refs):
    chunks, out_ref, acc = refs[:cols], refs[cols], refs[cols + 1]
    slots, side, block_size = sizes
    depth, listed, lines, _ = chunks[0].shape
    parity = LANES // block_size
    step = 4 if listed % 4 == 0 else 1
    acc[...] = jnp.zeros_like(acc)
    for d in range(cols):
        def entries(at, carry, d=d):
            made = []
            for k in range(step):
                e = at * step + k
                rows = chunks[d][:, pl.ds(e, 1)].reshape(depth * lines, LANES)
                made.append(jnp.dot(
                    rows, panel_ref[second_ref[d * listed + e]], preferred_element_type=jnp.float32))
            for k in range(step):
                corner = corner_ref[d * listed + at * step + k]
                for i in range(depth):
                    for odd in range(parity):
                        where = pl.ds(corner + odd, lines, stride=parity)
                        acc[i, where, :] += made[k][
                            i * lines : (i + 1) * lines, odd * LANES : (odd + 1) * LANES]
            return carry

        lax.fori_loop(0, listed // step, entries, 0)

    half = side // 2
    corners = ((0, 0), (0, 1), (1, 1))
    for a, b in corners:
        at = (slice(a * half, (a + 1) * half), slice(b * half, (b + 1) * half))
        out_ref[at] = jnp.zeros((half, half), jnp.float32) if first else tile_ref[at]
    batch = 4

    def products(group, carry):
        wide = jnp.concatenate(
            [
                acc[i, pl.ds(pl.multiple_of((group * batch + k) * side, side), side), :].astype(jnp.bfloat16)
                for k in range(batch)
                for i in range(depth)
            ],
            axis=1,
        )
        for a, b in corners:
            at = (slice(a * half, (a + 1) * half), slice(b * half, (b + 1) * half))
            out_ref[at] += lax.dot_general(
                wide[a * half : (a + 1) * half], wide[b * half : (b + 1) * half],
                (((1,), (1,)), ((), ())), preferred_element_type=jnp.float32)
        return carry

    lax.fori_loop(0, slots // batch, products, 0)
    if scale is not None:
        for a, b in corners:
            at = (slice(a * half, (a + 1) * half), slice(b * half, (b + 1) * half))
            out_ref[at] = out_ref[at] * scale
        out_ref[half:, :half] = out_ref[:half, half:].T


def build(cols, sizes, first, scale, corner, second, panels, tile, chunks):
    slots, side, _ = sizes
    depth = chunks[0].shape[0]
    return pl.pallas_call(
        functools.partial(build_kernel, cols, sizes, first, scale),
        out_shape=jax.ShapeDtypeStruct((side, side), jnp.float32),
        in_specs=[SMEM, SMEM, VMEM, VMEM] + [VMEM] * cols,
        out_specs=VMEM,
        scratch_shapes=[pltpu.VMEM((depth, slots * side, LANES), jnp.float32)],
        compiler_params=pltpu.CompilerParams(vmem_limit_bytes=56 * 2**20),
        cost_estimate=pl.CostEstimate(flops=10**10, bytes_accessed=8 * 2**20, transcendentals=0),
        name="build_tile",
    )(corner, second, panels, tile, *chunks)


def reduce_kernel(cols, tile_ref, out_ref, landed, crossing, crossed, sends, recvs):
    me_row, me_col = lax.axis_index("row"), lax.axis_index("col")
    share = out_ref.shape[0]
    half = cols // 2
    opposite = lax.bitwise_xor(me_col, half)

    def rows_of(col):
        return pl.ds(pl.multiple_of(col * share, share), share)

    barrier = pltpu.get_barrier_semaphore()
    for d in range(1, half + 1):
        pl.semaphore_signal(
            barrier, inc=1, device_id=(me_row, lax.bitwise_xor(me_col, d)), device_id_type=MESH)
    pl.semaphore_wait(barrier, half)
    near = []
    for side in (1, 0):
        for d in range(1, half):
            peer = lax.bitwise_xor(me_col, d)
            near.append(pltpu.make_async_remote_copy(
                tile_ref.at[rows_of(lax.bitwise_xor(peer, side * half))], landed.at[side, d - 1],
                sends.at[side, d - 1], recvs.at[side, d - 1], device_id=(me_row, peer), device_id_type=MESH))
            near[-1].start()
    total = tile_ref[rows_of(opposite), :]
    for d in range(1, half):
        near[d - 1].wait_recv()
        total = total + landed[1, d - 1]
    crossing[...] = total
    total = tile_ref[rows_of(me_col), :]
    out_ref[...] = total
    far = pltpu.make_async_remote_copy(
        crossing, crossed, sends.at[0, half - 1], recvs.at[0, half - 1],
        device_id=(me_row, opposite), device_id_type=MESH)
    far.start()
    for d in range(1, half):
        near[half - 2 + d].wait_recv()
        total = total + landed[0, d - 1]
    far.wait_recv()
    out_ref[...] = total + crossed[...]
    for copy in near:
        copy.wait_send()
    far.wait_send()


def reduce_tiles(cols, tile):
    side = tile.shape[0]
    half = cols // 2
    return pl.pallas_call(
        functools.partial(reduce_kernel, cols),
        out_shape=jax.ShapeDtypeStruct((side // cols, side), jnp.float32),
        in_specs=[VMEM],
        out_specs=VMEM,
        scratch_shapes=[
            pltpu.VMEM((2, half - 1, side // cols, side), jnp.float32),
            pltpu.VMEM((side // cols, side), jnp.float32),
            pltpu.VMEM((side // cols, side), jnp.float32),
            pltpu.SemaphoreType.DMA((2, half)),
            pltpu.SemaphoreType.DMA((2, half)),
        ],
        compiler_params=pltpu.CompilerParams(collective_id=1, has_side_effects=True),
        name="reduce_tiles",
    )(tile)


def on_device(integrals, block_list, p_slot, metric, density_panel, pattern):
    rows, cols = lax.axis_size("row"), lax.axis_size("col")
    me_col = lax.axis_index("col")
    owned_slots, block_size = metric.shape[0], metric.shape[1]
    listed = integrals.shape[0]
    panel_width = density_panel.shape[1]
    slots = owned_slots * cols
    side = MB * block_size
    mine = block_size // cols
    depth = DEPTH if mine % DEPTH == 0 else 1
    phases = mine // depth
    metrics, panels_col, patterns_col, lists_col = spread(
        "col", cols, 0, (metric, density_panel, pattern.reshape(1, -1), block_list))
    metrics = metrics.reshape(slots, block_size, block_size)
    slot_match = block_list[:, 2][:, None] == jnp.arange(slots, dtype=jnp.int32)[None, :]
    slot_ids = jnp.sum(jnp.where(slot_match, p_slot[None, :], 0), axis=1)

    offsets = jnp.arange(cols, dtype=jnp.int32)
    peers = lax.bitwise_xor(offsets, me_col)
    places = jnp.arange(block_size, dtype=jnp.int32)
    sent = []
    for phase in range(phases):
        wanted = (peers[:, None] * mine + phase * depth + jnp.arange(depth, dtype=jnp.int32)).reshape(-1)
        pick = (wanted[:, None] == places[None, :]).astype(jnp.bfloat16)
        outgoing = apply_metric(cols, slot_ids, pick, metrics, integrals)
        arrived = [outgoing[0]]
        for d in range(1, cols):
            arrived.append(lax.ppermute(outgoing[d], "col", [(c, c ^ d) for c in range(cols)]))
        sent.append(arrived)
        if phase == 0:
            panels_col, patterns_col, lists_col, _ = lax.optimization_barrier(
                (panels_col, patterns_col, lists_col, outgoing[1]))

    panel_all, pattern_all = spread("row", rows, 2, (panels_col, patterns_col))
    panel_all = panel_all.reshape(-1, panel_width)
    panel_all = jnp.where(pattern_all.reshape(-1, 1) > 0, panel_all, jnp.zeros_like(panel_all))
    lists_in = jnp.sum(
        jnp.where((peers[:, None] == offsets[None, :])[:, :, None, None], lists_col[None], 0), axis=1)
    lists_in = lists_in.reshape(cols * listed, 3)
    match_in = lists_in[:, 2][:, None] == jnp.arange(slots, dtype=jnp.int32)[None, :]
    slots_in = jnp.sum(jnp.where(match_in, p_slot[None, :], 0), axis=1)
    corner = slots_in * side + (lists_in[:, 0] - lax.axis_index("row") * MB) * block_size
    second = lists_in[:, 1]
    parity = LANES // block_size
    blocks = panel_all.reshape(-1, block_size, panel_width)
    panels = jnp.concatenate(
        [
            jnp.pad(blocks, ((0, 0), (0, 0), (k * panel_width, (parity - 1 - k) * panel_width)))
            for k in range(parity)
        ],
        axis=1,
    )
    tile = jnp.zeros((8, LANES), jnp.float32)
    for phase in range(phases):
        last = phase == phases - 1
        scale = 1.0 / (slots * block_size * panel_width) if last else None
        tile = build(
            cols, (slots, side, block_size), phase == 0, scale, corner, second, panels, tile, sent[phase])
    return reduce_tiles(cols, tile)


def solution(mesh):
    placed = (
        P(("row", "col"), None, None),
        P(("row", "col"), None),
        P(),
        P("col", None, None),
        P(("row", "col"), None),
        P(("row", "col")),
    )
    return jax.shard_map(
        on_device, mesh=mesh, in_specs=placed, out_specs=P(("row", "col"), None), check_vma=False
    )
```
